32 devices in a mesh: chan: 4 (over x, core), rad: 8 (over z, y).
Axes of the slice: x: 2, y: 2, z: 4, core: 2. Of those that a mesh axis runs over, the one named last changes fastest.
Arguments:
- psi: float32 [2, 768, 128, 128], P(None, 'chan', 'rad'), may hold values from -6 to 6
- k_prev: float32 [2, 768, 128, 128], P(None, 'chan', 'rad'), may hold values from -6 to 6
- gaunt: bfloat16 [4, 768, 768], replicated, may hold values from -0.875 to 0.875
- dipole: bfloat16 [768, 768], replicated, may hold values from -0.875 to 0.875
- kinetic: float32 [128, 128], replicated, as said below
- chan_l: int32 [768, 2], P('chan'), may hold values from 0 to 23
- field_amp: float32 [1], replicated, may hold values from 0.02 to 0.1
Outputs:
- deriv: float32 [2, 768, 128, 128], P(None, 'chan', 'rad')
The draws below stay inside these ranges and needn't reach their ends.
Inputs may be any that keep to these rules, and one draw needn't show every extreme that they name: `kinetic`: symmetric; zero where the row's and the column's blocks of 16 indices are more than one block apart.
All inputs are finite; a program needn't handle non-finite values.
Results may differ from the reference program's by a relative error of at most 0.00037.
Values may be sent and summed in bfloat16 or wider, within the bound.
A program may use at most 64 MiB of HBM per device.

```python
import jax
import jax.numpy as jnp
from jax import lax

C = 768
R_DEV = 16
LAM = 4
NR = 128


def draw_kinetic(key, part):
    spread = 1.0 / (3.0 * R_DEV) ** 0.5
    raw = jax.random.normal(key, (NR, NR), jnp.float32) * spread
    blocks = jnp.arange(NR, dtype=jnp.int32) // R_DEV
    band = (jnp.abs(blocks[:, None] - blocks[None, :]) <= 1).astype(jnp.float32)
    return (raw + raw.T) * 0.5 * band + 2.0 * jnp.eye(NR, dtype=jnp.float32)


def touch_ends(drawn, stream_key, low, largest):
    place = [jax.random.randint(jax.random.fold_in(stream_key, axis), (), 0, length) for axis, length in enumerate(drawn.shape)]
    widest = drawn.shape.index(max(drawn.shape))
    next_to = place[:widest] + [(place[widest] + 1) % drawn.shape[widest]] + place[widest + 1:]
    return drawn.at[tuple(place)].set(low).at[tuple(next_to)].set(largest)


def levels(stream_key, extent, split, smallest, high):
    def one(position, blocks):
        draws = jax.random.uniform(jax.random.fold_in(jax.random.fold_in(stream_key, 6), position), (blocks,), jnp.float32, smallest / len(split), high / len(split))
        return jnp.repeat(jnp.exp(draws), extent[position] // blocks).reshape((-1,) + (1,) * (len(extent) - position - 1))

    gain = one(*split[0])
    for cut in split[1:]:
        gain = gain * one(*cut)
    return gain


def gaussian(own_key, shape, deviation, bound, shards=(), kind=jnp.bfloat16):
    array = jax.random.normal(own_key, shape, jnp.float32) * deviation
    if len(shards) > 0:
        array = levels(own_key, shape, shards, -0.22, 0.18) * array
    return jnp.clip(array, min=-bound, max=bound).astype(kind)


def setup_inputs(seed: int = 0) -> dict:
    splits = jax.random.split(jax.random.key(seed), 8)
    return {
        "psi": gaussian(splits[0], (2, C, NR, NR), 1.0, 6.0, ((1, 4), (2, 8)), jnp.float32),
        "k_prev": gaussian(splits[1], (2, C, NR, NR), 1.0, 6.0, ((1, 4), (2, 8)), jnp.float32),
        "gaunt": gaussian(splits[2], (LAM, C, C), (C // 16) ** -0.5, 0.875),
        "dipole": gaussian(splits[3], (C, C), (C // 16) ** -0.5, 0.875),
        "kinetic": draw_kinetic(jax.random.fold_in(splits[7], 71), 0),
        "chan_l": touch_ends(jax.random.randint(splits[5], (C, 2), 0, 24), jax.random.fold_in(splits[5], 1), 0, 23).astype(jnp.int32),
        "field_amp": jnp.clip(jax.random.uniform(splits[6], (1,), jnp.float32, 0.02, 0.1), 0.02, 0.1),
    }


def radial_grid(count):
    return 1.0 + 8.0 * jnp.arange(count, dtype=jnp.float32) / count


def reference(psi, k_prev, gaunt, dipole, kinetic, chan_l, field_amp):
    highest = lax.Precision.HIGHEST
    section = psi + 0.5 * k_prev
    sent = section.astype(jnp.bfloat16)
    radius = radial_grid(NR)
    along_r1 = jnp.einsum('ij,acjk->acik', kinetic, section, precision=highest)
    along_r2 = jnp.einsum('acij,kj->acik', section, kinetic, precision=highest)
    lvals = chan_l.astype(jnp.float32)
    first_l = lvals[:, 0] * (lvals[:, 0] + 1.0)
    second_l = lvals[:, 1] * (lvals[:, 1] + 1.0)
    potential = (first_l[:, None, None] / (2.0 * radius * radius)[None, :, None]
                 + second_l[:, None, None] / (2.0 * radius * radius)[None, None, :]
                 - 2.0 / radius[None, :, None] - 2.0 / radius[None, None, :])
    first_r = jnp.broadcast_to(radius[:, None], (NR, NR)).reshape(-1)
    second_r = jnp.broadcast_to(radius[None, :], (NR, NR)).reshape(-1)
    far = jnp.maximum(first_r, second_r)
    near = jnp.minimum(first_r, second_r)
    inverse = 1.0 / far
    ratio = near * inverse
    flat = sent.reshape(2, C, NR * NR).astype(jnp.float32)
    power = inverse
    total = jnp.zeros((2, C, NR * NR), jnp.float32)
    for order in range(LAM):
        mixed = jnp.einsum('cd,adq->acq', gaunt[order].astype(jnp.float32), flat, precision=highest)
        total = total + power[None, None, :] * mixed
        power = power * ratio
    mixed = jnp.einsum('cd,adq->acq', dipole.astype(jnp.float32), flat, precision=highest)
    total = total + (field_amp[0] * (first_r + second_r))[None, None, :] * mixed
    coupled = total.astype(jnp.bfloat16).reshape(2, C, NR, NR)
    ham = along_r1 + along_r2 + potential[None] * section + coupled.astype(jnp.float32)
    return jnp.stack([ham[1], -ham[0]])
```

```python
import functools

import jax
import jax.numpy as jnp
from jax import lax
from jax.experimental import pallas as pl
from jax.experimental.pallas import tpu as pltpu
from jax.sharding import PartitionSpec as P


def extended(array, sides, width):
    for axis, dim in sides:
        peers, length = (lax.axis_size(axis), array.shape[dim])
        up = [(i, (i + 1) % peers) for i in range(peers - 1)]
        down = [(j, i) for i, j in up]
        last = lax.slice_in_dim(array, length - width, length, axis=dim)
        initial = lax.slice_in_dim(array, 0, width, axis=dim)
        before = lax.ppermute(last, axis, up)
        after = lax.ppermute(initial, axis, down)
        array = jnp.concatenate([before, array, after], axis=dim)
    return array


def on_device(psi, k_prev, gaunt, dipole, kinetic, chan_l, field_amp):
    highest = lax.Precision.HIGHEST
    section = psi + 0.5 * k_prev
    local_chan = section.shape[1]
    rows = section.shape[2]
    width = section.shape[3]
    rad_at = lax.axis_index("rad")
    first_r = (
        1.0 + 8.0 * (rad_at * rows + jnp.arange(rows, dtype=jnp.int32)).astype(jnp.float32) / width
    )
    second_r = 1.0 + 8.0 * jnp.arange(width, dtype=jnp.float32) / width
    along_r2 = jnp.einsum("acij,kj->acik", section, kinetic, precision=highest)
    padded = extended(section.astype(jnp.bfloat16), (("rad", 2),), rows).astype(section.dtype)
    band = lax.dynamic_slice_in_dim(kinetic, rad_at * rows, rows, 0)
    widened = jnp.pad(band, ((0, 0), (rows, rows)))
    local_band = lax.dynamic_slice_in_dim(widened, rad_at * rows, 3 * rows, 1)
    along_r1 = jnp.einsum("ij,acjk->acik", local_band, padded, precision=highest)
    lvals = chan_l.astype(jnp.float32)
    first_l = lvals[:, 0] * (lvals[:, 0] + 1.0)
    second_l = lvals[:, 1] * (lvals[:, 1] + 1.0)
    potential = (
        first_l[:, None, None] / (2.0 * first_r * first_r)[None, :, None]
        + second_l[:, None, None] / (2.0 * second_r * second_r)[None, None, :]
        - 2.0 / first_r[None, :, None]
        - 2.0 / second_r[None, None, :]
    )
    sent = section.astype(jnp.bfloat16).reshape(2, local_chan, rows * width)
    chan_at = lax.axis_index("chan")
    block = lax.all_to_all(sent, "chan", split_axis=2, concat_axis=1, tiled=True)
    count = block.shape[2]
    place = chan_at * count + jnp.arange(count, dtype=jnp.int32)
    row_r = 1.0 + 8.0 * (rad_at * rows + place // width).astype(jnp.float32) / width
    col_r = 1.0 + 8.0 * (place % width).astype(jnp.float32) / width
    far = jnp.maximum(row_r, col_r)
    near = jnp.minimum(row_r, col_r)
    inverse = 1.0 / far
    ratio = near * inverse
    power = inverse
    total = jnp.zeros(block.shape, jnp.float32)
    for order in range(gaunt.shape[0]):
        mixed = jnp.einsum("cd,adq->acq", gaunt[order], block, preferred_element_type=jnp.float32)
        total = total + power[None, None, :] * mixed
        power = power * ratio
    mixed = jnp.einsum("cd,adq->acq", dipole, block, preferred_element_type=jnp.float32)
    total = total + (field_amp[0] * (row_r + col_r))[None, None, :] * mixed
    coupled = lax.all_to_all(
        total.astype(jnp.bfloat16), "chan", split_axis=1, concat_axis=2, tiled=True
    )
    coupled = coupled.reshape(coupled.shape[0], local_chan, rows, width)
    ham = along_r1 + along_r2 + potential[None] * section + coupled.astype(jnp.float32)
    return jnp.stack([ham[1], -ham[0]])


MESH = pl.DeviceIdType.MESH
GROUP = 16


def split_bf16(value):
    high = value.astype(jnp.bfloat16)
    return high, (value - high.astype(jnp.float32)).astype(jnp.bfloat16)


def fused_kernel(
    peers,
    rads,
    psi,
    k_prev,
    gaunt,
    dipole,
    kin,
    chan_l,
    field,
    out,
    pbuf,
    kbuf,
    sec,
    xg,
    halo,
    acc,
    acc1,
    weights,
    wr1,
    kk,
    lmul,
    langle,
    load_sem,
    weight_sem,
    xs,
    xr,
    cs,
    cr,
    fs,
    fr,
    ys,
    yr,
    zs,
    zr,
    store_sem,
):
    rows, chans, lanes = sec.shape
    width = lanes // 2
    orders = weights.shape[0]
    chips = peers // 2
    halves = rows // 8
    quarter = rows // 4
    span = chans // 4
    chan_at = lax.axis_index("chan")
    rad_at = lax.axis_index("rad")
    core = chan_at % 2
    chip = chan_at // 2
    partner = chan_at + 1 - 2 * core
    minor = rad_at % 2
    other = rad_at + 1 - 2 * minor
    ahead = rad_at + 2 - 4 * minor
    behind = rad_at - 2 + 4 * minor
    has_ahead = jnp.logical_and(ahead >= 0, ahead < rads)
    has_behind = jnp.logical_and(behind >= 0, behind < rads)
    near_slot = 1 - minor
    far_slot = minor

    def block(owner):
        return pl.ds(pl.multiple_of(owner * chans, GROUP), chans)

    def chip_peer(step):
        return lax.rem(chip + step, chips) * 2 + core

    def chip_source(step):
        return lax.rem(chip - step + chips, chips) * 2 + core

    def load(which, half, part):
        source, target = ((psi, pbuf), (k_prev, kbuf))[which]
        return pltpu.make_async_copy(
            source.at[part, :, pl.ds(half * 8, 8), :],
            target.at[half, part],
            load_sem.at[which, half, part],
        )

    def load_weight(order):
        source = gaunt.at[order] if order < orders - 1 else dipole
        return pltpu.make_async_copy(
            source.at[block(chan_at), :], weights.at[order], weight_sem.at[order]
        )

    def store(half, part):
        return pltpu.make_async_copy(
            pbuf.at[half, part],
            out.at[part, :, pl.ds(half * 8, 8), :],
            store_sem.at[half, part],
        )

    def remote(ref, send, recv, target):
        return pltpu.make_async_remote_copy(
            src_ref=ref[0],
            dst_ref=ref[1],
            send_sem=send,
            recv_sem=recv,
            device_id=target,
            device_id_type=MESH,
        )

    def chip_copy(step, row, owner):
        view = xg.at[row, block(owner), :]
        return remote(
            (view, view), xs.at[step - 1, row], xr.at[step - 1, row], {"chan": chip_peer(step)}
        )

    def core_copy(row, owner):
        view = xg.at[row, block(owner), :]
        return remote((view, view), cs.at[row], cr.at[row], {"chan": partner})

    def relay_copy(step, row, owner):
        view = xg.at[row, block(owner), :]
        return remote((view, view), fs.at[step - 1, row], fr.at[step - 1, row], {"chan": partner})

    def piece(index):
        row = pl.ds(pl.multiple_of((index // 4) * quarter, quarter), quarter)
        first = pl.multiple_of((index % 4) * span, GROUP)
        return row, first

    def own_piece(index):
        row, first = piece(index)
        start = pl.multiple_of(chan_at * chans + first, GROUP)
        return xg.at[row, pl.ds(start, span), :]

    def halo_piece(slot, index):
        row, first = piece(index)
        return halo.at[slot, row, pl.ds(first, span), :]

    def side_copy(index):
        return remote(
            (own_piece(index), halo_piece(minor, index)), ys.at[index], yr.at[index], {"rad": other}
        )

    def far_copy(index):
        return remote(
            (halo_piece(near_slot, index), halo_piece(minor, index)),
            zs.at[index],
            zr.at[index],
            {"rad": ahead},
        )

    for half in range(halves):
        for part in range(2):
            for which in range(2):
                load(which, half, part).start()
    for order in range(orders):
        load_weight(order).start()

    barrier = pltpu.get_barrier_semaphore()
    for step in range(1, chips):
        pl.semaphore_signal(
            barrier, inc=1, device_id={"chan": chip_peer(step)}, device_id_type=MESH
        )
    pl.semaphore_signal(barrier, inc=1, device_id={"chan": partner}, device_id_type=MESH)
    pl.semaphore_signal(barrier, inc=1, device_id={"rad": other}, device_id_type=MESH)

    @pl.when(has_ahead)
    def _():
        pl.semaphore_signal(barrier, inc=1, device_id={"rad": ahead}, device_id_type=MESH)

    @pl.when(has_behind)
    def _():
        pl.semaphore_signal(barrier, inc=1, device_id={"rad": behind}, device_id_type=MESH)

    pl.semaphore_wait(
        barrier, chips + 1 + has_ahead.astype(jnp.int32) + has_behind.astype(jnp.int32)
    )

    def send_row(row):
        for step in range(1, chips):
            chip_copy(step, row, chan_at).start()
        core_copy(row, chan_at).start()

    def send_side(first):
        for index in range(4):
            side_copy(first * 4 + index).start()

    for half in range(halves):
        for part in range(2):
            for which in range(2):
                load(which, half, part).wait()
        for row in range(half * 8, half * 8 + 8):
            for part in range(2):
                place = (pl.ds(row % 8, chans, stride=8), slice(None))
                value = (
                    pbuf.at[half, part].reshape(chans * 8, width)[place]
                    + 0.5 * kbuf.at[half, part].reshape(chans * 8, width)[place]
                )
                cut = slice(part * width, (part + 1) * width)
                sec[row, :, cut] = value
                xg[row, block(chan_at), cut] = value.astype(jnp.bfloat16)
            if row >= 1:
                send_row(row - 1)
                if row % quarter == 0:
                    send_side(row // quarter - 1)

    kin_high, kin_low = split_bf16(kin[...])
    both = jnp.concatenate([kin_high, kin_low], axis=1)
    kk[0:width, :] = both
    kk[width : 2 * width, :] = both
    send_row(rows - 1)
    send_side(3)

    band = kin[pl.ds(pl.multiple_of(rad_at * rows, rows), rows), :]
    size = rows * GROUP
    tall = jnp.broadcast_to(band[:, None, :], (rows, GROUP, width)).reshape(size, width)
    tall_high, tall_low = split_bf16(tall)
    at_row = lax.broadcasted_iota(jnp.int32, (size, size), 0)
    at_col = lax.broadcasted_iota(jnp.int32, (size, size), 1)
    same = (at_row % GROUP) == (at_col % GROUP)
    from_j = lax.broadcasted_iota(jnp.int32, (width, size), 0)
    to_col = lax.broadcasted_iota(jnp.int32, (width, size), 1)
    for side in range(3):
        pick = from_j == (rad_at + side - 1) * rows + to_col // GROUP
        pick = jnp.where(pick, 1.0, 0.0).astype(jnp.bfloat16)
        for level, source in enumerate((tall_high, tall_low)):
            wide = jnp.dot(source, pick, preferred_element_type=jnp.float32)
            wr1[side, level * size : (level + 1) * size, :] = jnp.where(same, wide, 0.0).astype(
                jnp.bfloat16
            )

    @pl.when(jnp.logical_not(has_behind))
    def _():
        halo[far_slot] = jnp.zeros(halo.shape[1:], halo.dtype)

    second_r = 1.0 + 8.0 * (
        lax.broadcasted_iota(jnp.int32, (1, lanes), 1) % width
    ).astype(jnp.float32) / width
    inner_r = second_r[:, :width]
    lvals = chan_l[...].astype(jnp.float32)
    lvals = lvals * (lvals + 1.0)
    lmul[...] = jnp.broadcast_to(lvals[:, 0:1], (chans, width))
    langle[...] = lvals[:, 1:2] / (2.0 * inner_r * inner_r) - 2.0 / inner_r

    def radius(row):
        place = jnp.full((1, lanes), rad_at * rows + row, jnp.int32)
        return 1.0 + 8.0 * place.astype(jnp.float32) / width

    for order in range(orders):
        load_weight(order).wait()

    def local_row(row):
        first_r = radius(row)[:, :width]
        scale = 1.0 / (2.0 * first_r * first_r)
        shift = 2.0 / first_r
        potential = lmul[...] * scale + langle[...] - shift
        for part in range(2):
            cut = slice(part * width, (part + 1) * width)
            value = sec[row, :, cut]
            high = xg[row, block(chan_at), cut]
            low = (value - high.astype(jnp.float32)).astype(jnp.bfloat16)
            both = jnp.dot(
                jnp.concatenate([high, low], axis=1), kk[...], preferred_element_type=jnp.float32
            )
            acc[row, :, cut] = both[:, :width] + both[:, width:] + potential * value

    def mix(side, value):
        both = jnp.dot(wr1[side], value, preferred_element_type=jnp.float32)
        return both[:size] + both[size:]

    def own_group(index):
        first = pl.multiple_of(index * GROUP, GROUP)
        start = pl.multiple_of(chan_at * chans + first, GROUP)
        high = xg[:, pl.ds(start, GROUP), :].reshape(size, lanes)
        value = sec[:, pl.ds(first, GROUP), :].reshape(size, lanes)
        low = (value - high.astype(jnp.float32)).astype(jnp.bfloat16)
        total = mix(1, high) + jnp.dot(
            wr1[1, 0:size, :], low, preferred_element_type=jnp.float32
        )
        acc1[:, pl.ds(first, GROUP), :] = total.reshape(rows, GROUP, lanes)

    def side_group(index):
        first = pl.multiple_of(index * GROUP, GROUP)
        cut = pl.ds(first, GROUP)
        total = mix(0, halo[0, :, cut, :].reshape(size, lanes)) + mix(
            2, halo[1, :, cut, :].reshape(size, lanes)
        )
        acc1[:, cut, :] = acc1[:, cut, :] + total.reshape(rows, GROUP, lanes)

    def couple(row):
        first_r = radius(row)
        inverse = 1.0 / jnp.maximum(first_r, second_r)
        ratio = jnp.minimum(first_r, second_r) * inverse
        factors = [inverse]
        for _ in range(orders - 2):
            factors.append(factors[-1] * ratio)
        factors.append(field[0] * (first_r + second_r))
        step = chans // 2
        for first in range(0, chans, step):
            total = jnp.zeros((step, lanes), jnp.float32)
            for order in range(orders):
                total = total + factors[order] * jnp.dot(
                    weights[order, first : first + step, :],
                    xg[row],
                    preferred_element_type=jnp.float32,
                )
            acc[row, first : first + step, :] = acc[row, first : first + step, :] + total.astype(
                jnp.bfloat16
            ).astype(jnp.float32)

    def take_row(row):
        core_copy(row, partner).wait_recv()
        for step in range(1, chips):
            relay_copy(step, row, chip_source(step) + 1 - 2 * core).wait_recv()
        couple(row)

    def main(row, carry):
        @pl.when(row < chans // GROUP)
        def _():
            own_group(row)

        local_row(row)
        for step in range(1, chips):
            chip_copy(step, row, chip_source(step)).wait_recv()
            relay_copy(step, row, chip_source(step)).start()
        side_copy(row).wait_recv()

        @pl.when(has_ahead)
        def _():
            far_copy(row).start()

        @pl.when(row >= 1)
        def _():
            take_row(row - 1)

        return carry

    lax.fori_loop(0, rows, main, 0)
    take_row(rows - 1)

    @pl.when(has_behind)
    def _():
        for index in range(rows):
            far_copy(index).wait_recv()

    def finish(index, carry):
        side_group(index)
        return carry

    lax.fori_loop(0, chans // GROUP, finish, 0)

    for half in range(halves):
        for row in range(half * 8, half * 8 + 8):
            value = acc[row] + acc1[row]
            place = (pl.ds(row % 8, chans, stride=8), slice(None))
            pbuf.at[half, 0].reshape(chans * 8, width)[place] = value[:, width:]
            pbuf.at[half, 1].reshape(chans * 8, width)[place] = -value[:, :width]
        for part in range(2):
            store(half, part).start()

    def drain(row, carry):
        for step in range(1, chips):
            chip_copy(step, row, chan_at).wait_send()
            relay_copy(step, row, chip_source(step)).wait_send()
        core_copy(row, chan_at).wait_send()
        side_copy(row).wait_send()

        @pl.when(has_ahead)
        def _():
            far_copy(row).wait_send()

        return carry

    lax.fori_loop(0, rows, drain, 0)
    for half in range(halves):
        for part in range(2):
            store(half, part).wait()


def device_step(peers, rads, psi, k_prev, gaunt, dipole, kinetic, chan_l, field_amp):
    _, chans, rows, width = psi.shape
    fits = (
        chans % (4 * GROUP) == 0
        and rows == GROUP
        and peers % 2 == 0
        and rads % 2 == 0
        and width == rads * rows
        and width == 128
    )
    if not fits:
        return on_device(psi, k_prev, gaunt, dipole, kinetic, chan_l, field_amp)
    orders = gaunt.shape[0] + 1
    chips = peers // 2
    lanes = 2 * width
    size = rows * GROUP
    f32, bf16, dma = (jnp.float32, jnp.bfloat16, pltpu.SemaphoreType.DMA)
    anywhere = pl.BlockSpec(memory_space=pl.ANY)
    vmem = pl.BlockSpec(memory_space=pltpu.VMEM)
    return pl.pallas_call(
        functools.partial(fused_kernel, peers, rads),
        out_shape=jax.ShapeDtypeStruct(psi.shape, f32),
        in_specs=[anywhere] * 4 + [vmem, vmem, pl.BlockSpec(memory_space=pltpu.SMEM)],
        out_specs=anywhere,
        scratch_shapes=[
            pltpu.VMEM((rows // 8, 2, chans, 8, width), f32),
            pltpu.VMEM((rows // 8, 2, chans, 8, width), f32),
            pltpu.VMEM((rows, chans, lanes), f32),
            pltpu.VMEM((rows, peers * chans, lanes), bf16),
            pltpu.VMEM((2, rows, chans, lanes), bf16),
            pltpu.VMEM((rows, chans, lanes), f32),
            pltpu.VMEM((rows, chans, lanes), f32),
            pltpu.VMEM((orders, chans, peers * chans), bf16),
            pltpu.VMEM((3, 2 * size, size), bf16),
            pltpu.VMEM((lanes, lanes), bf16),
            pltpu.VMEM((chans, width), f32),
            pltpu.VMEM((chans, width), f32),
            dma((2, rows // 8, 2)),
            dma((orders,)),
            dma((chips - 1, rows)),
            dma((chips - 1, rows)),
            dma((rows,)),
            dma((rows,)),
            dma((chips - 1, rows)),
            dma((chips - 1, rows)),
            dma((rows,)),
            dma((rows,)),
            dma((rows,)),
            dma((rows,)),
            dma((rows // 8, 2)),
        ],
        compiler_params=pltpu.CompilerParams(
            collective_id=0, has_side_effects=True, vmem_limit_bytes=60 * 1024 * 1024
        ),
    )(psi, k_prev, gaunt, dipole, kinetic, chan_l, field_amp)


def solution(mesh):
    placed = (
        P(None, "chan", "rad", None),
        P(None, "chan", "rad", None),
        P(),
        P(),
        P(),
        P("chan", None),
        P(),
    )
    return jax.shard_map(
        functools.partial(device_step, mesh.shape["chan"], mesh.shape["rad"]),
        mesh=mesh,
        in_specs=placed,
        out_specs=P(None, "chan", "rad", None),
        check_vma=False,
    )
```

```python
import functools

import jax
import jax.numpy as jnp
from jax import lax
from jax.experimental import pallas as pl
from jax.experimental.pallas import tpu as pltpu
from jax.sharding import PartitionSpec as P


def extended(array, sides, width):
    for axis, dim in sides:
        peers, length = (lax.axis_size(axis), array.shape[dim])
        up = [(i, (i + 1) % peers) for i in range(peers - 1)]
        down = [(j, i) for i, j in up]
        last = lax.slice_in_dim(array, length - width, length, axis=dim)
        initial = lax.slice_in_dim(array, 0, width, axis=dim)
        before = lax.ppermute(last, axis, up)
        after = lax.ppermute(initial, axis, down)
        array = jnp.concatenate([before, array, after], axis=dim)
    return array


def on_device(psi, k_prev, gaunt, dipole, kinetic, chan_l, field_amp):
    highest = lax.Precision.HIGHEST
    section = psi + 0.5 * k_prev
    local_chan = section.shape[1]
    rows = section.shape[2]
    width = section.shape[3]
    rad_at = lax.axis_index("rad")
    first_r = (
        1.0 + 8.0 * (rad_at * rows + jnp.arange(rows, dtype=jnp.int32)).astype(jnp.float32) / width
    )
    second_r = 1.0 + 8.0 * jnp.arange(width, dtype=jnp.float32) / width
    along_r2 = jnp.einsum("acij,kj->acik", section, kinetic, precision=highest)
    padded = extended(section.astype(jnp.bfloat16), (("rad", 2),), rows).astype(section.dtype)
    band = lax.dynamic_slice_in_dim(kinetic, rad_at * rows, rows, 0)
    widened = jnp.pad(band, ((0, 0), (rows, rows)))
    local_band = lax.dynamic_slice_in_dim(widened, rad_at * rows, 3 * rows, 1)
    along_r1 = jnp.einsum("ij,acjk->acik", local_band, padded, precision=highest)
    lvals = chan_l.astype(jnp.float32)
    first_l = lvals[:, 0] * (lvals[:, 0] + 1.0)
    second_l = lvals[:, 1] * (lvals[:, 1] + 1.0)
    potential = (
        first_l[:, None, None] / (2.0 * first_r * first_r)[None, :, None]
        + second_l[:, None, None] / (2.0 * second_r * second_r)[None, None, :]
        - 2.0 / first_r[None, :, None]
        - 2.0 / second_r[None, None, :]
    )
    sent = section.astype(jnp.bfloat16).reshape(2, local_chan, rows * width)
    chan_at = lax.axis_index("chan")
    block = lax.all_to_all(sent, "chan", split_axis=2, concat_axis=1, tiled=True)
    count = block.shape[2]
    place = chan_at * count + jnp.arange(count, dtype=jnp.int32)
    row_r = 1.0 + 8.0 * (rad_at * rows + place // width).astype(jnp.float32) / width
    col_r = 1.0 + 8.0 * (place % width).astype(jnp.float32) / width
    far = jnp.maximum(row_r, col_r)
    near = jnp.minimum(row_r, col_r)
    inverse = 1.0 / far
    ratio = near * inverse
    power = inverse
    total = jnp.zeros(block.shape, jnp.float32)
    for order in range(gaunt.shape[0]):
        mixed = jnp.einsum("cd,adq->acq", gaunt[order], block, preferred_element_type=jnp.float32)
        total = total + power[None, None, :] * mixed
        power = power * ratio
    mixed = jnp.einsum("cd,adq->acq", dipole, block, preferred_element_type=jnp.float32)
    total = total + (field_amp[0] * (row_r + col_r))[None, None, :] * mixed
    coupled = lax.all_to_all(
        total.astype(jnp.bfloat16), "chan", split_axis=1, concat_axis=2, tiled=True
    )
    coupled = coupled.reshape(coupled.shape[0], local_chan, rows, width)
    ham = along_r1 + along_r2 + potential[None] * section + coupled.astype(jnp.float32)
    return jnp.stack([ham[1], -ham[0]])


MESH = pl.DeviceIdType.MESH
GROUP = 16


def split_bf16(value):
    high = value.astype(jnp.bfloat16)
    return high, (value - high.astype(jnp.float32)).astype(jnp.bfloat16)


def fused_kernel(
    peers,
    rads,
    psi,
    k_prev,
    gaunt,
    dipole,
    kin,
    chan_l,
    field,
    out,
    pbuf,
    kbuf,
    sec,
    xg,
    halo,
    acc,
    acc1,
    weights,
    wr1,
    kk,
    lmul,
    langle,
    load_sem,
    weight_sem,
    hs,
    hr,
    xs,
    xr,
    cs,
    cr,
    fs,
    fr,
    ys,
    yr,
    zs,
    zr,
    store_sem,
):
    rows, chans, lanes = sec.shape
    width = lanes // 2
    orders = weights.shape[0]
    chips = peers // 2
    groups = chans // GROUP
    lead = rows // 4
    chan_at = lax.axis_index("chan")
    rad_at = lax.axis_index("rad")
    core = chan_at % 2
    chip = chan_at // 2
    partner = chan_at + 1 - 2 * core
    minor = rad_at % 2
    other = rad_at + 1 - 2 * minor
    ahead = rad_at + 2 - 4 * minor
    behind = rad_at - 2 + 4 * minor
    has_ahead = jnp.logical_and(ahead >= 0, ahead < rads)
    has_behind = jnp.logical_and(behind >= 0, behind < rads)
    near_slot = 1 - minor
    far_slot = minor

    def block(owner):
        return pl.ds(pl.multiple_of(owner * chans, GROUP), chans)

    def cut_of(group):
        return pl.ds(pl.multiple_of(group * GROUP, GROUP), GROUP)

    def block_cut(owner, group):
        return pl.ds(pl.multiple_of(owner * chans + group * GROUP, GROUP), GROUP)

    def chip_peer(step):
        return lax.rem(chip + step, chips) * 2 + core

    def chip_source(step):
        return lax.rem(chip - step + chips, chips) * 2 + core

    def load(which, group):
        source, target = ((psi, pbuf), (k_prev, kbuf))[which]
        return pltpu.make_async_copy(
            source.at[:, cut_of(group), :, :],
            target.at[:, cut_of(group), :, :],
            load_sem.at[which, group],
        )

    def load_weight(order):
        source = gaunt.at[order] if order < orders - 1 else dipole
        return pltpu.make_async_copy(
            source.at[block(chan_at), :], weights.at[order], weight_sem.at[order]
        )

    def store(group):
        return pltpu.make_async_copy(
            pbuf.at[:, cut_of(group), :, :], out.at[:, cut_of(group), :, :], store_sem.at[group]
        )

    def remote(source, target, send, recv, device):
        return pltpu.make_async_remote_copy(
            src_ref=source,
            dst_ref=target,
            send_sem=send,
            recv_sem=recv,
            device_id=device,
            device_id_type=MESH,
        )

    def lead_copy(step, group, owner):
        view = xg.at[0:lead, block_cut(owner, group), :]
        device = {"chan": chip_peer(step)}
        return remote(view, view, hs.at[step - 1, group], hr.at[step - 1, group], device)

    def chip_copy(step, row, owner):
        view = xg.at[row, block(owner), :]
        device = {"chan": chip_peer(step)}
        return remote(view, view, xs.at[step - 1, row], xr.at[step - 1, row], device)

    def core_copy(index, owner):
        view = xg.at[index * lead : (index + 1) * lead, block(owner), :]
        return remote(view, view, cs.at[index], cr.at[index], {"chan": partner})

    def relay_lead(step, owner):
        view = xg.at[0:lead, block(owner), :]
        return remote(view, view, fs.at[step - 1, 0], fr.at[step - 1, 0], {"chan": partner})

    def relay_copy(step, row, owner):
        view = xg.at[row, block(owner), :]
        return remote(view, view, fs.at[step - 1, row], fr.at[step - 1, row], {"chan": partner})

    def side_copy(group):
        source = xg.at[:, block_cut(chan_at, group), :]
        target = halo.at[minor, :, cut_of(group), :]
        return remote(source, target, ys.at[group], yr.at[group], {"rad": other})

    def far_copy(group):
        source = halo.at[near_slot, :, cut_of(group), :]
        target = halo.at[minor, :, cut_of(group), :]
        return remote(source, target, zs.at[group], zr.at[group], {"rad": ahead})

    for group in range(groups):
        for which in range(2):
            load(which, group).start()
    for order in range(orders):
        load_weight(order).start()

    barrier = pltpu.get_barrier_semaphore()
    for step in range(1, chips):
        pl.semaphore_signal(
            barrier, inc=1, device_id={"chan": chip_peer(step)}, device_id_type=MESH
        )
    pl.semaphore_signal(barrier, inc=1, device_id={"chan": partner}, device_id_type=MESH)
    pl.semaphore_signal(barrier, inc=1, device_id={"rad": other}, device_id_type=MESH)

    @pl.when(has_ahead)
    def _():
        pl.semaphore_signal(barrier, inc=1, device_id={"rad": ahead}, device_id_type=MESH)

    @pl.when(has_behind)
    def _():
        pl.semaphore_signal(barrier, inc=1, device_id={"rad": behind}, device_id_type=MESH)

    def form(group):
        for which in range(2):
            load(which, group).wait()
        for part in range(2):
            first = pbuf.at[part].reshape(chans * rows, width)
            second = kbuf.at[part].reshape(chans * rows, width)
            cut = slice(part * width, (part + 1) * width)
            for row in range(rows):
                place = (pl.ds(group * GROUP * rows + row, GROUP, stride=rows), slice(None))
                value = first[place] + 0.5 * second[place]
                sec[row, cut_of(group), cut] = value
                xg[row, block_cut(chan_at, group), cut] = value.astype(jnp.bfloat16)

    def send_group(group):
        side_copy(group).start()
        for step in range(1, chips):
            lead_copy(step, group, chan_at).start()

    form(0)
    pl.semaphore_wait(
        barrier, chips + 1 + has_ahead.astype(jnp.int32) + has_behind.astype(jnp.int32)
    )

    def form_next(group, carry):
        form(group)
        send_group(group - 1)
        return carry

    lax.fori_loop(1, groups, form_next, 0)

    kin_high, kin_low = split_bf16(kin[...])
    both = jnp.concatenate([kin_high, kin_low], axis=1)
    kk[0:width, :] = both
    kk[width : 2 * width, :] = both
    send_group(groups - 1)
    for row in range(lead, rows):
        for step in range(1, chips):
            chip_copy(step, row, chan_at).start()
    for index in range(4):
        core_copy(index, chan_at).start()

    band = kin[pl.ds(pl.multiple_of(rad_at * rows, rows), rows), :]
    size = rows * GROUP
    tall = jnp.broadcast_to(band[:, None, :], (rows, GROUP, width)).reshape(size, width)
    tall_high, tall_low = split_bf16(tall)
    at_row = lax.broadcasted_iota(jnp.int32, (size, size), 0)
    at_col = lax.broadcasted_iota(jnp.int32, (size, size), 1)
    same = (at_row % GROUP) == (at_col % GROUP)
    from_j = lax.broadcasted_iota(jnp.int32, (width, size), 0)
    to_col = lax.broadcasted_iota(jnp.int32, (width, size), 1)
    for side in range(3):
        pick = from_j == (rad_at + side - 1) * rows + to_col // GROUP
        pick = jnp.where(pick, 1.0, 0.0).astype(jnp.bfloat16)
        for level, source in enumerate((tall_high, tall_low)):
            wide = jnp.dot(source, pick, preferred_element_type=jnp.float32)
            wr1[side, level * size : (level + 1) * size, :] = jnp.where(same, wide, 0.0).astype(
                jnp.bfloat16
            )

    @pl.when(jnp.logical_not(has_behind))
    def _():
        halo[far_slot] = jnp.zeros(halo.shape[1:], halo.dtype)

    second_r = 1.0 + 8.0 * (
        lax.broadcasted_iota(jnp.int32, (1, lanes), 1) % width
    ).astype(jnp.float32) / width
    inner_r = second_r[:, :width]
    lvals = chan_l[...].astype(jnp.float32).astype(jnp.bfloat16)
    first = lax.broadcasted_iota(jnp.int32, (2, lanes), 0)
    spread = first == lax.broadcasted_iota(jnp.int32, (2, lanes), 1) // width
    spread = jnp.where(spread, 1.0, 0.0).astype(jnp.bfloat16)
    lwide = lax.dot_general(
        lvals, spread, (((0,), (0,)), ((), ())), preferred_element_type=jnp.float32
    )
    lwide = lwide * (lwide + 1.0)
    lmul[...] = lwide[:, :width]
    langle[...] = lwide[:, width:] / (2.0 * inner_r * inner_r) - 2.0 / inner_r

    def radius(row):
        place = jnp.full((1, lanes), rad_at * rows + row, jnp.int32)
        return 1.0 + 8.0 * place.astype(jnp.float32) / width

    for order in range(orders):
        load_weight(order).wait()

    def local_row(row):
        first_r = radius(row)[:, :width]
        scale = 1.0 / (2.0 * first_r * first_r)
        shift = 2.0 / first_r
        potential = lmul[...] * scale + langle[...] - shift
        for part in range(2):
            cut = slice(part * width, (part + 1) * width)
            value = sec[row, :, cut]
            high = xg[row, block(chan_at), cut]
            low = (value - high.astype(jnp.float32)).astype(jnp.bfloat16)
            both = jnp.dot(
                jnp.concatenate([high, low], axis=1), kk[...], preferred_element_type=jnp.float32
            )
            acc[row, :, cut] = both[:, :width] + both[:, width:] + potential * value

    def mix(side, value):
        both = jnp.dot(wr1[side], value, preferred_element_type=jnp.float32)
        return both[:size] + both[size:]

    def own_group(index):
        first = pl.multiple_of(index * GROUP, GROUP)
        start = pl.multiple_of(chan_at * chans + first, GROUP)
        high = xg[:, pl.ds(start, GROUP), :].reshape(size, lanes)
        value = sec[:, pl.ds(first, GROUP), :].reshape(size, lanes)
        low = (value - high.astype(jnp.float32)).astype(jnp.bfloat16)
        total = mix(1, high) + jnp.dot(
            wr1[1, 0:size, :], low, preferred_element_type=jnp.float32
        )
        acc1[:, pl.ds(first, GROUP), :] = total.reshape(rows, GROUP, lanes)

    def side_group(index):
        first = pl.multiple_of(index * GROUP, GROUP)
        cut = pl.ds(first, GROUP)
        total = mix(0, halo[0, :, cut, :].reshape(size, lanes)) + mix(
            2, halo[1, :, cut, :].reshape(size, lanes)
        )
        acc1[:, cut, :] = acc1[:, cut, :] + total.reshape(rows, GROUP, lanes)

    def couple(row):
        first_r = radius(row)
        inverse = 1.0 / jnp.maximum(first_r, second_r)
        ratio = jnp.minimum(first_r, second_r) * inverse
        factors = [inverse]
        for _ in range(orders - 2):
            factors.append(factors[-1] * ratio)
        factors.append(field[0] * (first_r + second_r))
        step = chans // 2
        for first in range(0, chans, step):
            total = jnp.zeros((step, lanes), jnp.float32)
            for order in range(orders):
                total = total + factors[order] * jnp.dot(
                    weights[order, first : first + step, :],
                    xg[row],
                    preferred_element_type=jnp.float32,
                )
            acc[row, first : first + step, :] = acc[row, first : first + step, :] + total.astype(
                jnp.bfloat16
            ).astype(jnp.float32)

    def relay(row):
        for step in range(1, chips):
            chip_copy(step, row, chip_source(step)).wait_recv()
            relay_copy(step, row, chip_source(step)).start()

    def take_row(row):
        for step in range(1, chips):
            relay_copy(step, row, chip_source(step) + 1 - 2 * core).wait_recv()
        couple(row)

    def pass_side(group):
        side_copy(group).wait_recv()

        @pl.when(has_ahead)
        def _():
            far_copy(group).start()

    def take_side(group):
        @pl.when(has_behind)
        def _():
            far_copy(group).wait_recv()

        side_group(group)

    early = groups // 4

    def begin(index, carry):
        own_group(index)
        for place in range(4):
            local_row(index * 4 + place)
        pass_side(index)
        return carry

    lax.fori_loop(0, early, begin, 0)
    for step in range(1, chips):
        for group in range(groups):
            lead_copy(step, group, chip_source(step)).wait_recv()
        relay_lead(step, chip_source(step)).start()
    for index in range(4):
        core_copy(index, partner).wait_recv()
    for step in range(1, chips):
        relay_lead(step, chip_source(step) + 1 - 2 * core).wait_recv()

    def main(index, carry):
        @pl.when(index + early < groups)
        def _():
            own_group(index + early)

        @pl.when(jnp.logical_and(index >= lead, index < 2 * lead))
        def _():
            local_row(index + rows - 2 * lead)

        late = index - index // 4

        @pl.when(index % 4 != 3)
        def _():
            pass_side(early + late)

        relay(lead + index)

        @pl.when(index < lead)
        def _():
            couple(index)

        @pl.when(index % 4 != 3)
        def _():
            take_side(late)

        @pl.when(index >= 1)
        def _():
            take_row(lead + index - 1)

        return carry

    lax.fori_loop(0, rows - lead, main, 0)
    take_row(rows - 1)

    def finish(group, carry):
        @pl.when(group >= groups - early)
        def _():
            take_side(group)

        cut = cut_of(group)
        first = pbuf.at[0].reshape(chans * rows, width)
        second = pbuf.at[1].reshape(chans * rows, width)
        for row in range(rows):
            value = acc[row, cut, :] + acc1[row, cut, :]
            place = (pl.ds(group * GROUP * rows + row, GROUP, stride=rows), slice(None))
            first[place] = value[:, width:]
            second[place] = -value[:, :width]
        store(group).start()
        return carry

    lax.fori_loop(0, groups, finish, 0)

    def drain_row(row, carry):
        for step in range(1, chips):
            chip_copy(step, row, chan_at).wait_send()
            relay_copy(step, row, chip_source(step)).wait_send()
        return carry

    def drain_group(group, carry):
        for step in range(1, chips):
            lead_copy(step, group, chan_at).wait_send()
        side_copy(group).wait_send()

        @pl.when(has_ahead)
        def _():
            far_copy(group).wait_send()

        store(group).wait()
        return carry

    for index in range(4):
        core_copy(index, chan_at).wait_send()
    for step in range(1, chips):
        relay_lead(step, chip_source(step)).wait_send()
    lax.fori_loop(lead, rows, drain_row, 0)
    lax.fori_loop(0, groups, drain_group, 0)


def device_step(peers, rads, psi, k_prev, gaunt, dipole, kinetic, chan_l, field_amp):
    _, chans, rows, width = psi.shape
    fits = (
        chans == 3 * 4 * GROUP
        and rows == GROUP
        and peers % 2 == 0
        and rads % 2 == 0
        and width == rads * rows
        and width == 128
    )
    if not fits:
        return on_device(psi, k_prev, gaunt, dipole, kinetic, chan_l, field_amp)
    orders = gaunt.shape[0] + 1
    chips = peers // 2
    groups = chans // GROUP
    lanes = 2 * width
    size = rows * GROUP
    f32, bf16, dma = (jnp.float32, jnp.bfloat16, pltpu.SemaphoreType.DMA)
    main_memory = pl.BlockSpec(memory_space=pltpu.HBM)
    vmem = pl.BlockSpec(memory_space=pltpu.VMEM)
    psi, k_prev, gaunt, dipole = (
        pltpu.with_memory_space_constraint(value, pltpu.HBM)
        for value in (psi, k_prev, gaunt, dipole)
    )
    return pl.pallas_call(
        functools.partial(fused_kernel, peers, rads),
        out_shape=jax.ShapeDtypeStruct(psi.shape, f32),
        in_specs=[main_memory] * 4 + [vmem, vmem, pl.BlockSpec(memory_space=pltpu.SMEM)],
        out_specs=pl.BlockSpec(memory_space=pl.ANY),
        scratch_shapes=[
            pltpu.VMEM((2, chans, rows, width), f32),
            pltpu.VMEM((2, chans, rows, width), f32),
            pltpu.VMEM((rows, chans, lanes), f32),
            pltpu.VMEM((rows, peers * chans, lanes), bf16),
            pltpu.VMEM((2, rows, chans, lanes), bf16),
            pltpu.VMEM((rows, chans, lanes), f32),
            pltpu.VMEM((rows, chans, lanes), f32),
            pltpu.VMEM((orders, chans, peers * chans), bf16),
            pltpu.VMEM((3, 2 * size, size), bf16),
            pltpu.VMEM((lanes, lanes), bf16),
            pltpu.VMEM((chans, width), f32),
            pltpu.VMEM((chans, width), f32),
            dma((2, groups)),
            dma((orders,)),
            dma((chips - 1, groups)),
            dma((chips - 1, groups)),
            dma((chips - 1, rows)),
            dma((chips - 1, rows)),
            dma((4,)),
            dma((4,)),
            dma((chips - 1, rows)),
            dma((chips - 1, rows)),
            dma((groups,)),
            dma((groups,)),
            dma((groups,)),
            dma((groups,)),
            dma((groups,)),
        ],
        compiler_params=pltpu.CompilerParams(
            collective_id=0, has_side_effects=True, vmem_limit_bytes=36 * 1024 * 1024
        ),
    )(psi, k_prev, gaunt, dipole, kinetic, chan_l.T, field_amp)


def solution(mesh):
    placed = (
        P(None, "chan", "rad", None),
        P(None, "chan", "rad", None),
        P(),
        P(),
        P(),
        P("chan", None),
        P(),
    )
    return jax.shard_map(
        functools.partial(device_step, mesh.shape["chan"], mesh.shape["rad"]),
        mesh=mesh,
        in_specs=placed,
        out_specs=P(None, "chan", "rad", None),
        check_vma=False,
    )
```

```python
import functools

import jax
import jax.numpy as jnp
from jax import lax
from jax.experimental import pallas as pl
from jax.experimental.pallas import tpu as pltpu
from jax.sharding import PartitionSpec as P


def extended(array, sides, width):
    for axis, dim in sides:
        peers, length = (lax.axis_size(axis), array.shape[dim])
        up = [(i, (i + 1) % peers) for i in range(peers - 1)]
        down = [(j, i) for i, j in up]
        last = lax.slice_in_dim(array, length - width, length, axis=dim)
        initial = lax.slice_in_dim(array, 0, width, axis=dim)
        before = lax.ppermute(last, axis, up)
        after = lax.ppermute(initial, axis, down)
        array = jnp.concatenate([before, array, after], axis=dim)
    return array


def on_device(psi, k_prev, gaunt, dipole, kinetic, chan_l, field_amp):
    highest = lax.Precision.HIGHEST
    section = psi + 0.5 * k_prev
    local_chan = section.shape[1]
    rows = section.shape[2]
    width = section.shape[3]
    rad_at = lax.axis_index("rad")
    first_r = (
        1.0 + 8.0 * (rad_at * rows + jnp.arange(rows, dtype=jnp.int32)).astype(jnp.float32) / width
    )
    second_r = 1.0 + 8.0 * jnp.arange(width, dtype=jnp.float32) / width
    along_r2 = jnp.einsum("acij,kj->acik", section, kinetic, precision=highest)
    padded = extended(section.astype(jnp.bfloat16), (("rad", 2),), rows).astype(section.dtype)
    band = lax.dynamic_slice_in_dim(kinetic, rad_at * rows, rows, 0)
    widened = jnp.pad(band, ((0, 0), (rows, rows)))
    local_band = lax.dynamic_slice_in_dim(widened, rad_at * rows, 3 * rows, 1)
    along_r1 = jnp.einsum("ij,acjk->acik", local_band, padded, precision=highest)
    lvals = chan_l.astype(jnp.float32)
    first_l = lvals[:, 0] * (lvals[:, 0] + 1.0)
    second_l = lvals[:, 1] * (lvals[:, 1] + 1.0)
    potential = (
        first_l[:, None, None] / (2.0 * first_r * first_r)[None, :, None]
        + second_l[:, None, None] / (2.0 * second_r * second_r)[None, None, :]
        - 2.0 / first_r[None, :, None]
        - 2.0 / second_r[None, None, :]
    )
    sent = section.astype(jnp.bfloat16).reshape(2, local_chan, rows * width)
    chan_at = lax.axis_index("chan")
    block = lax.all_to_all(sent, "chan", split_axis=2, concat_axis=1, tiled=True)
    count = block.shape[2]
    place = chan_at * count + jnp.arange(count, dtype=jnp.int32)
    row_r = 1.0 + 8.0 * (rad_at * rows + place // width).astype(jnp.float32) / width
    col_r = 1.0 + 8.0 * (place % width).astype(jnp.float32) / width
    far = jnp.maximum(row_r, col_r)
    near = jnp.minimum(row_r, col_r)
    inverse = 1.0 / far
    ratio = near * inverse
    power = inverse
    total = jnp.zeros(block.shape, jnp.float32)
    for order in range(gaunt.shape[0]):
        mixed = jnp.einsum("cd,adq->acq", gaunt[order], block, preferred_element_type=jnp.float32)
        total = total + power[None, None, :] * mixed
        power = power * ratio
    mixed = jnp.einsum("cd,adq->acq", dipole, block, preferred_element_type=jnp.float32)
    total = total + (field_amp[0] * (row_r + col_r))[None, None, :] * mixed
    coupled = lax.all_to_all(
        total.astype(jnp.bfloat16), "chan", split_axis=1, concat_axis=2, tiled=True
    )
    coupled = coupled.reshape(coupled.shape[0], local_chan, rows, width)
    ham = along_r1 + along_r2 + potential[None] * section + coupled.astype(jnp.float32)
    return jnp.stack([ham[1], -ham[0]])


MESH = pl.DeviceIdType.MESH
GROUP = 16


def split_bf16(value):
    high = value.astype(jnp.bfloat16)
    return high, (value - high.astype(jnp.float32)).astype(jnp.bfloat16)


def fused_kernel(
    peers,
    rads,
    psi,
    k_prev,
    gaunt,
    dipole,
    kin_main,
    chan_main,
    field,
    out,
    kin,
    chan_l,
    pbuf,
    kbuf,
    sec,
    xg,
    halo,
    acc,
    acc1,
    weights,
    wr1,
    kk,
    lmul,
    langle,
    load_sem,
    weight_sem,
    hs,
    hr,
    xs,
    xr,
    cs,
    cr,
    fs,
    fr,
    ys,
    yr,
    zs,
    zr,
    small_sem,
):
    rows, chans, lanes = sec.shape
    width = lanes // 2
    orders = weights.shape[0]
    chips = peers // 2
    groups = chans // GROUP
    lead = rows // 4
    chan_at = lax.axis_index("chan")
    rad_at = lax.axis_index("rad")
    core = chan_at % 2
    chip = chan_at // 2
    partner = chan_at + 1 - 2 * core
    minor = rad_at % 2
    other = rad_at + 1 - 2 * minor
    ahead = rad_at + 2 - 4 * minor
    behind = rad_at - 2 + 4 * minor
    has_ahead = jnp.logical_and(ahead >= 0, ahead < rads)
    has_behind = jnp.logical_and(behind >= 0, behind < rads)
    near_slot = 1 - minor
    far_slot = minor

    def block(owner):
        return pl.ds(pl.multiple_of(owner * chans, GROUP), chans)

    def cut_of(group):
        return pl.ds(pl.multiple_of(group * GROUP, GROUP), GROUP)

    def block_cut(owner, group):
        return pl.ds(pl.multiple_of(owner * chans + group * GROUP, GROUP), GROUP)

    def chip_peer(step):
        return lax.rem(chip + step, chips) * 2 + core

    def chip_source(step):
        return lax.rem(chip - step + chips, chips) * 2 + core

    def load(which, group):
        source, target = ((psi, pbuf), (k_prev, kbuf))[which]
        return pltpu.make_async_copy(
            source.at[:, cut_of(group), :, :],
            target.at[:, cut_of(group), :, :],
            load_sem.at[which, group],
        )

    def load_weight(order):
        source = gaunt.at[order] if order < orders - 1 else dipole
        return pltpu.make_async_copy(
            source.at[block(chan_at), :], weights.at[order], weight_sem.at[order]
        )

    def remote(source, target, send, recv, device):
        return pltpu.make_async_remote_copy(
            src_ref=source,
            dst_ref=target,
            send_sem=send,
            recv_sem=recv,
            device_id=device,
            device_id_type=MESH,
        )

    def lead_copy(step, group, owner):
        view = xg.at[0:lead, block_cut(owner, group), :]
        device = {"chan": chip_peer(step)}
        return remote(view, view, hs.at[step - 1, group], hr.at[step - 1, group], device)

    def chip_copy(step, row, owner):
        view = xg.at[row, block(owner), :]
        device = {"chan": chip_peer(step)}
        return remote(view, view, xs.at[step - 1, row], xr.at[step - 1, row], device)

    def core_copy(index, owner):
        view = xg.at[index * lead : (index + 1) * lead, block(owner), :]
        return remote(view, view, cs.at[index], cr.at[index], {"chan": partner})

    def relay_lead(step, owner):
        view = xg.at[0:lead, block(owner), :]
        return remote(view, view, fs.at[step - 1, 0], fr.at[step - 1, 0], {"chan": partner})

    def relay_copy(step, row, owner):
        view = xg.at[row, block(owner), :]
        return remote(view, view, fs.at[step - 1, row], fr.at[step - 1, row], {"chan": partner})

    def half_of(half):
        return slice(half * (rows // 2), (half + 1) * (rows // 2))

    def side_copy(group, half):
        source = xg.at[half_of(half), block_cut(chan_at, group), :]
        target = halo.at[minor, half_of(half), cut_of(group), :]
        return remote(source, target, ys.at[half, group], yr.at[half, group], {"rad": other})

    def far_copy(group, half):
        source = halo.at[near_slot, half_of(half), cut_of(group), :]
        target = halo.at[minor, half_of(half), cut_of(group), :]
        return remote(source, target, zs.at[half, group], zr.at[half, group], {"rad": ahead})

    small = [
        pltpu.make_async_copy(kin_main, kin, small_sem.at[0]),
        pltpu.make_async_copy(chan_main, chan_l, small_sem.at[1]),
    ]
    depth = groups
    for group in range(depth):
        for which in range(2):
            load(which, group).start()

    barrier = pltpu.get_barrier_semaphore()
    for step in range(1, chips):
        pl.semaphore_signal(
            barrier, inc=1, device_id={"chan": chip_peer(step)}, device_id_type=MESH
        )
    pl.semaphore_signal(barrier, inc=1, device_id={"chan": partner}, device_id_type=MESH)
    pl.semaphore_signal(barrier, inc=1, device_id={"rad": other}, device_id_type=MESH)

    @pl.when(has_ahead)
    def _():
        pl.semaphore_signal(barrier, inc=1, device_id={"rad": ahead}, device_id_type=MESH)

    @pl.when(has_behind)
    def _():
        pl.semaphore_signal(barrier, inc=1, device_id={"rad": behind}, device_id_type=MESH)

    def form(group):
        for which in range(2):
            load(which, group).wait()

        for part in range(2):
            first = pbuf.at[part].reshape(chans * rows, width)
            second = kbuf.at[part].reshape(chans * rows, width)
            cut = slice(part * width, (part + 1) * width)
            for row in range(rows):
                place = (pl.ds(group * GROUP * rows + row, GROUP, stride=rows), slice(None))
                value = first[place] + 0.5 * second[place]
                sec[row, cut_of(group), cut] = value
                xg[row, block_cut(chan_at, group), cut] = value.astype(jnp.bfloat16)

    def send_group(group):
        for half in range(2):
            side_copy(group, half).start()
        for step in range(1, chips):
            lead_copy(step, group, chan_at).start()

    form(jnp.int32(0))
    pl.semaphore_wait(
        barrier, chips + 1 + has_ahead.astype(jnp.int32) + has_behind.astype(jnp.int32)
    )

    def form_next(group, carry):
        form(group)
        send_group(group - 1)
        return carry

    lax.fori_loop(1, groups, form_next, 0)
    for copy in small:
        copy.start()
    for order in range(orders):
        load_weight(order).start()

    send_group(groups - 1)
    for row in range(lead, rows):
        for step in range(1, chips):
            chip_copy(step, row, chan_at).start()
    for index in range(4):
        core_copy(index, chan_at).start()

    for copy in small:
        copy.wait()
    kin_high, kin_low = split_bf16(kin[...])
    both = jnp.concatenate([kin_high, kin_low], axis=1)
    kk[0:width, :] = both
    kk[width : 2 * width, :] = both

    band = kin[pl.ds(pl.multiple_of(rad_at * rows, rows), rows), :]
    size = rows * GROUP
    tall = jnp.broadcast_to(band[:, None, :], (rows, GROUP, width)).reshape(size, width)
    tall_high, tall_low = split_bf16(tall)
    at_row = lax.broadcasted_iota(jnp.int32, (size, size), 0)
    at_col = lax.broadcasted_iota(jnp.int32, (size, size), 1)
    same = (at_row % GROUP) == (at_col % GROUP)
    from_j = lax.broadcasted_iota(jnp.int32, (width, size), 0)
    to_col = lax.broadcasted_iota(jnp.int32, (width, size), 1)
    for side in range(3):
        pick = from_j == (rad_at + side - 1) * rows + to_col // GROUP
        pick = jnp.where(pick, 1.0, 0.0).astype(jnp.bfloat16)
        for level, source in enumerate((tall_high, tall_low)):
            wide = jnp.dot(source, pick, preferred_element_type=jnp.float32)
            wr1[side, level * size : (level + 1) * size, :] = jnp.where(same, wide, 0.0).astype(
                jnp.bfloat16
            )

    @pl.when(jnp.logical_not(has_behind))
    def _():
        halo[far_slot] = jnp.zeros(halo.shape[1:], halo.dtype)

    second_r = 1.0 + 8.0 * (
        lax.broadcasted_iota(jnp.int32, (1, lanes), 1) % width
    ).astype(jnp.float32) / width
    inner_r = second_r[:, :width]
    lvals = chan_l[...].astype(jnp.float32).astype(jnp.bfloat16)
    first = lax.broadcasted_iota(jnp.int32, (2, lanes), 0)
    spread = first == lax.broadcasted_iota(jnp.int32, (2, lanes), 1) // width
    spread = jnp.where(spread, 1.0, 0.0).astype(jnp.bfloat16)
    lwide = lax.dot_general(
        lvals, spread, (((0,), (0,)), ((), ())), preferred_element_type=jnp.float32
    )
    lwide = lwide * (lwide + 1.0)
    lmul[...] = lwide[:, :width]
    langle[...] = lwide[:, width:] / (2.0 * inner_r * inner_r) - 2.0 / inner_r

    def radius(row):
        place = jnp.full((1, lanes), rad_at * rows + row, jnp.int32)
        return 1.0 + 8.0 * place.astype(jnp.float32) / width

    for order in range(orders):
        load_weight(order).wait()

    def local_row(row):
        first_r = radius(row)[:, :width]
        scale = 1.0 / (2.0 * first_r * first_r)
        shift = 2.0 / first_r
        potential = lmul[...] * scale + langle[...] - shift
        for part in range(2):
            cut = slice(part * width, (part + 1) * width)
            value = sec[row, :, cut]
            high = xg[row, block(chan_at), cut]
            low = (value - high.astype(jnp.float32)).astype(jnp.bfloat16)
            both = jnp.dot(
                jnp.concatenate([high, low], axis=1), kk[...], preferred_element_type=jnp.float32
            )
            acc[row, :, cut] = both[:, :width] + both[:, width:] + potential * value

    def mix(side, value):
        both = jnp.dot(wr1[side], value, preferred_element_type=jnp.float32)
        return both[:size] + both[size:]

    def own_group(index):
        first = pl.multiple_of(index * GROUP, GROUP)
        start = pl.multiple_of(chan_at * chans + first, GROUP)
        high = xg[:, pl.ds(start, GROUP), :].reshape(size, lanes)
        value = sec[:, pl.ds(first, GROUP), :].reshape(size, lanes)
        low = (value - high.astype(jnp.float32)).astype(jnp.bfloat16)
        total = mix(1, high) + jnp.dot(
            wr1[1, 0:size, :], low, preferred_element_type=jnp.float32
        )
        acc1[:, pl.ds(first, GROUP), :] = total.reshape(rows, GROUP, lanes)

    def side_group(index):
        first = pl.multiple_of(index * GROUP, GROUP)
        cut = pl.ds(first, GROUP)
        total = mix(0, halo[0, :, cut, :].reshape(size, lanes)) + mix(
            2, halo[1, :, cut, :].reshape(size, lanes)
        )
        acc1[:, cut, :] = acc1[:, cut, :] + total.reshape(rows, GROUP, lanes)

    def couple(row):
        first_r = radius(row)
        inverse = 1.0 / jnp.maximum(first_r, second_r)
        ratio = jnp.minimum(first_r, second_r) * inverse
        factors = [inverse]
        for _ in range(orders - 2):
            factors.append(factors[-1] * ratio)
        factors.append(field[0] * (first_r + second_r))
        step = chans // 2
        for first in range(0, chans, step):
            total = jnp.zeros((step, lanes), jnp.float32)
            for order in range(orders):
                total = total + factors[order] * jnp.dot(
                    weights[order, first : first + step, :],
                    xg[row],
                    preferred_element_type=jnp.float32,
                )
            acc[row, first : first + step, :] = acc[row, first : first + step, :] + total.astype(
                jnp.bfloat16
            ).astype(jnp.float32)

    def relay(row):
        for step in range(1, chips):
            chip_copy(step, row, chip_source(step)).wait_recv()
            relay_copy(step, row, chip_source(step)).start()

    def take_row(row):
        for step in range(1, chips):
            relay_copy(step, row, chip_source(step) + 1 - 2 * core).wait_recv()
        couple(row)

    def pass_side(group):
        for half in range(2):
            side_copy(group, half).wait_recv()

            @pl.when(has_ahead)
            def _():
                far_copy(group, half).start()

    def take_side(group):
        @pl.when(has_behind)
        def _():
            for half in range(2):
                far_copy(group, half).wait_recv()

        side_group(group)

    early = groups // 4

    def begin(index, carry):
        own_group(index)
        for place in range(4):
            local_row(index * 4 + place)
        pass_side(index)
        return carry

    lax.fori_loop(0, early, begin, 0)
    for step in range(1, chips):
        for group in range(groups):
            lead_copy(step, group, chip_source(step)).wait_recv()
        relay_lead(step, chip_source(step)).start()
    for index in range(4):
        core_copy(index, partner).wait_recv()
    for step in range(1, chips):
        relay_lead(step, chip_source(step) + 1 - 2 * core).wait_recv()

    def main(index, carry):
        @pl.when(index + early < groups)
        def _():
            own_group(index + early)

        @pl.when(jnp.logical_and(index >= lead, index < 2 * lead))
        def _():
            local_row(index + rows - 2 * lead)

        late = early + index - index // 4

        @pl.when(index % 4 != 3)
        def _():
            pass_side(late)

        relay(lead + index)

        @pl.when(index < lead)
        def _():
            couple(index)

        @pl.when(index % 4 != 3)
        def _():
            take_side(late - early)

        @pl.when(index >= 1)
        def _():
            take_row(lead + index - 1)

        return carry

    lax.fori_loop(0, rows - lead, main, 0)

    def merge(group, some_rows):
        cut = cut_of(group)
        first = out.at[0].reshape(chans * rows, width)
        second = out.at[1].reshape(chans * rows, width)
        for row in some_rows:
            value = acc[row, cut, :] + acc1[row, cut, :]
            place = (pl.ds(group * GROUP * rows + row, GROUP, stride=rows), slice(None))
            first[place] = value[:, width:]
            second[place] = -value[:, :width]

    def merge_most(group, carry):
        merge(group, range(rows - 1))
        return carry

    def merge_last(group, carry):
        merge(group, range(rows - 1, rows))
        return carry

    def merge_side(group, carry):
        take_side(group)
        merge(group, range(rows))
        return carry

    lax.fori_loop(0, groups - early, merge_most, 0)
    take_row(rows - 1)
    lax.fori_loop(0, groups - early, merge_last, 0)
    lax.fori_loop(groups - early, groups, merge_side, 0)

    def drain_row(row, carry):
        for step in range(1, chips):
            chip_copy(step, row, chan_at).wait_send()
            relay_copy(step, row, chip_source(step)).wait_send()
        return carry

    def drain_group(group, carry):
        for step in range(1, chips):
            lead_copy(step, group, chan_at).wait_send()
        for half in range(2):
            side_copy(group, half).wait_send()

        @pl.when(has_ahead)
        def _():
            for half in range(2):
                far_copy(group, half).wait_send()

        return carry

    for index in range(4):
        core_copy(index, chan_at).wait_send()
    for step in range(1, chips):
        relay_lead(step, chip_source(step)).wait_send()
    lax.fori_loop(lead, rows, drain_row, 0)
    lax.fori_loop(0, groups, drain_group, 0)


def device_step(peers, rads, psi, k_prev, gaunt, dipole, kinetic, chan_l, field_amp):
    _, chans, rows, width = psi.shape
    fits = (
        chans == 3 * 4 * GROUP
        and rows == GROUP
        and peers % 2 == 0
        and rads % 2 == 0
        and width == rads * rows
        and width == 128
    )
    if not fits:
        return on_device(psi, k_prev, gaunt, dipole, kinetic, chan_l, field_amp)
    orders = gaunt.shape[0] + 1
    chips = peers // 2
    groups = chans // GROUP
    lanes = 2 * width
    size = rows * GROUP
    f32, bf16, dma = (jnp.float32, jnp.bfloat16, pltpu.SemaphoreType.DMA)
    main_memory = pl.BlockSpec(memory_space=pltpu.HBM)
    vmem = pl.BlockSpec(memory_space=pltpu.VMEM)
    psi, k_prev, gaunt, dipole, kinetic, chan_l = (
        pltpu.with_memory_space_constraint(value, pltpu.HBM)
        for value in (psi, k_prev, gaunt, dipole, kinetic, chan_l.T)
    )
    return pl.pallas_call(
        functools.partial(fused_kernel, peers, rads),
        out_shape=jax.ShapeDtypeStruct(psi.shape, f32),
        in_specs=[main_memory] * 6 + [pl.BlockSpec(memory_space=pltpu.SMEM)],
        out_specs=vmem,
        scratch_shapes=[
            pltpu.VMEM(kinetic.shape, f32),
            pltpu.VMEM((2, chans), jnp.int32),
            pltpu.VMEM((2, chans, rows, width), f32),
            pltpu.VMEM((2, chans, rows, width), f32),
            pltpu.VMEM((rows, chans, lanes), f32),
            pltpu.VMEM((rows, peers * chans, lanes), bf16),
            pltpu.VMEM((2, rows, chans, lanes), bf16),
            pltpu.VMEM((rows, chans, lanes), f32),
            pltpu.VMEM((rows, chans, lanes), f32),
            pltpu.VMEM((orders, chans, peers * chans), bf16),
            pltpu.VMEM((3, 2 * size, size), bf16),
            pltpu.VMEM((lanes, lanes), bf16),
            pltpu.VMEM((chans, width), f32),
            pltpu.VMEM((chans, width), f32),
            dma((2, groups)),
            dma((orders,)),
            dma((chips - 1, groups)),
            dma((chips - 1, groups)),
            dma((chips - 1, rows)),
            dma((chips - 1, rows)),
            dma((4,)),
            dma((4,)),
            dma((chips - 1, rows)),
            dma((chips - 1, rows)),
            dma((2, groups)),
            dma((2, groups)),
            dma((2, groups)),
            dma((2, groups)),
            dma((2,)),
        ],
        compiler_params=pltpu.CompilerParams(
            collective_id=0, has_side_effects=True, vmem_limit_bytes=36 * 1024 * 1024
        ),
    )(psi, k_prev, gaunt, dipole, kinetic, chan_l, field_amp)


def solution(mesh):
    placed = (
        P(None, "chan", "rad", None),
        P(None, "chan", "rad", None),
        P(),
        P(),
        P(),
        P("chan", None),
        P(),
    )
    return jax.shard_map(
        functools.partial(device_step, mesh.shape["chan"], mesh.shape["rad"]),
        mesh=mesh,
        in_specs=placed,
        out_specs=P(None, "chan", "rad", None),
        check_vma=False,
    )
```
